32 devices in a mesh: dp: 4 (over y, x), seq: 8 (over z, core).
Axes of the slice: x: 2, y: 2, z: 4, core: 2. Of those that a mesh axis runs over, the one named last changes fastest.
Arguments:
- section_input: bfloat16 [16384, 1536], P(('dp', 'seq')), parts along dimension 0, may hold values from -6 to 6
- conv_gain: float32 [1536], replicated, may hold values from 0.1 to 1.9
- conv_weight: bfloat16 [5, 1536, 1536], replicated, may hold values from -0.0625 to 0.0625
- conv_bias: float32 [1536], replicated, may hold values from -3 to 3
- attn_gain: float32 [1536], replicated, may hold values from 0.1 to 1.9
- q_weight: bfloat16 [1536, 1024], P('seq'), may hold values from -5 to 5
- kv_weight: bfloat16 [1536, 320], P('seq'), may hold values from -0.15625 to 0.15625
- o_weight: bfloat16 [1536, 1536], P('seq'), may hold values from -0.15625 to 0.15625
Outputs:
- skip: bfloat16 [8192, 1536], P(('dp', 'seq')), parts along dimension 0
- block_out: bfloat16 [8192, 1536], P(('dp', 'seq')), parts along dimension 0
The draws below stay inside these ranges and needn't reach their ends.
There are 4 independent parts, one for each index of `dp`. The reference program is written for one: setup_inputs(seed, part) draws one part's arguments, and reference() takes and returns one part's arrays. A program takes and returns all parts, laid end to end along the dimension named above; an argument that names none is the same for every part. Nothing has to cross between parts.
All inputs are finite; a program needn't handle non-finite values.
Results may differ from the reference program's by a relative error of at most 0.008.
The reference program's roundings to bfloat16 on the way count: a program that leaves them out, or rounds other values in their place, can miss the bound.
Values may be sent and summed in bfloat16 or wider, within the bound.
A program may use at most 192 MiB of HBM per device.

```python
import jax
import jax.numpy as jnp
from jax import lax

D = 1536
HEADS = 8
DK = 128
DV = 192
TAPS = 5
TOKENS = 2048
POSITIONS = 4096
HV = 1536


def draw_q_weight(key, part):
    scale_key = jax.random.fold_in(key, 11)
    entry_key = jax.random.fold_in(key, 12)
    lower, upper = (1.0, 4.0)
    head_scales = jnp.exp(jax.random.uniform(scale_key, (HEADS,), jnp.float32, jnp.log(lower), jnp.log(upper)))
    entries = jax.random.truncated_normal(entry_key, -4.0, 4.0, (D, HEADS * DK), jnp.float32)
    column_scales = jnp.repeat(head_scales, DK) / jnp.sqrt(jnp.float32(D))
    return (entries * column_scales[None, :]).astype(jnp.bfloat16)


def levels(key, dims, pieces, low, high):
    level = 1.0
    for position, blocks in pieces:
        steps = jax.random.uniform(jax.random.fold_in(jax.random.fold_in(key, 6), position), (blocks,), jnp.float32, low / len(pieces), high / len(pieces))
        level = level * jnp.repeat(jnp.exp(steps), dims[position] // blocks).reshape((-1,) + (1,) * (len(dims) - 1 - position))
    return level


def bell_draw(stream_key, shape, spread, most, pieces=(), kind=jnp.bfloat16):
    result = jax.random.normal(stream_key, shape, jnp.float32) * spread
    if len(pieces) > 0:
        result = levels(stream_key, shape, pieces, -0.22, 0.18) * result
    return jnp.clip(result, min=-most, max=most).astype(kind)


def setup_inputs(seed: int = 0, part: int = 0) -> dict:
    seeds = jax.random.split(jax.random.key(seed), 9)
    part_keys = jax.random.split(jax.random.fold_in(seeds[8], part), 9)
    return {
        "section_input": bell_draw(part_keys[0], (POSITIONS, D), 1.0, 6.0, ((0, 8),)),
        "conv_gain": jnp.clip(1.0 + 0.18 * jax.random.normal(seeds[1], (D,), jnp.float32), 0.1, 1.9),
        "conv_weight": bell_draw(seeds[2], (TAPS, D, D), (TAPS * D) ** -0.5, 0.0625),
        "conv_bias": bell_draw(seeds[3], (D,), 0.5, 3.0, (), jnp.float32),
        "attn_gain": jnp.clip(1.0 + 0.18 * jax.random.normal(seeds[4], (D,), jnp.float32), 0.1, 1.9),
        "q_weight": draw_q_weight(jax.random.fold_in(seeds[8], 71), part),
        "kv_weight": bell_draw(seeds[6], (D, DK + DV), D ** -0.5, 0.15625, ((0, 8),)),
        "o_weight": bell_draw(seeds[7], (HV, D), HV ** -0.5, 0.15625, ((0, 8),)),
    }


def rms_scale(rows, gain):
    values = rows.astype(jnp.float32)
    return values * lax.rsqrt(lax.optimization_barrier(jnp.mean(values * values, axis=-1, keepdims=True)) + 1e-06) * gain

def rotate(values, positions):
    half_size = values.shape[-1] // 2
    freqs = jnp.power(10000.0, -jnp.arange(half_size, dtype=jnp.float32) / half_size)
    angle = positions.astype(jnp.float32)[:, None] * freqs[None, :]
    if values.ndim == 3:
        angle = angle[:, None, :]
    cosine = jnp.cos(angle)
    sine = jnp.sin(angle)
    first = values[..., :half_size]
    second = values[..., half_size:]
    return jnp.concatenate([first * cosine - second * sine, second * cosine + first * sine], axis=-1)

def reference(section_input, conv_gain, conv_weight, conv_bias, attn_gain, q_weight, kv_weight, o_weight):
    activated = jax.nn.gelu(rms_scale(section_input, conv_gain), approximate=True).astype(jnp.bfloat16)
    reach = TAPS // 2
    padded = jnp.pad(activated, ((reach, reach), (0, 0)))
    conv = jnp.zeros((POSITIONS, D), jnp.float32) + conv_bias
    for kernel_tap in range(TAPS):
        conv = conv + jnp.dot(padded[kernel_tap:kernel_tap + POSITIONS], conv_weight[kernel_tap], preferred_element_type=jnp.float32)
    summed = section_input.astype(jnp.float32) + conv
    skip = lax.optimization_barrier(jnp.max(summed.reshape(TOKENS, 2, D), axis=1)).astype(jnp.bfloat16)
    normed = rms_scale(skip, attn_gain).astype(jnp.bfloat16)
    positions = jnp.arange(TOKENS, dtype=jnp.int32)
    queries = jnp.dot(normed, q_weight, preferred_element_type=jnp.float32).reshape(TOKENS, HEADS, DK)
    queries = rotate(queries, positions).astype(jnp.bfloat16)
    projected = jnp.dot(normed, kv_weight, preferred_element_type=jnp.float32)
    keys = rotate(projected[:, :DK], positions).astype(jnp.bfloat16)
    values = projected[:, DK:].astype(jnp.bfloat16)
    score_scale = DK ** (-0.5)

    def one_head(head_queries):
        scores = jnp.dot(head_queries, keys.T, preferred_element_type=jnp.float32) * score_scale
        peak = lax.optimization_barrier(jnp.max(scores, axis=-1, keepdims=True))
        weights = jnp.exp(scores - peak)
        total = lax.optimization_barrier(jnp.sum(weights, axis=-1, keepdims=True))
        return jnp.dot(weights.astype(jnp.bfloat16), values, preferred_element_type=jnp.float32) / total
    heads_out = lax.map(one_head, jnp.transpose(queries, (1, 0, 2)))
    mixed = jnp.transpose(heads_out, (1, 0, 2)).reshape(TOKENS, HV).astype(jnp.bfloat16)
    attended = jnp.dot(mixed, o_weight, preferred_element_type=jnp.float32)
    block_out = (skip.astype(jnp.float32) + attended).astype(jnp.bfloat16)
    return (skip, block_out)
```

```python
import functools

import jax
import jax.numpy as jnp
from jax import lax
from jax.experimental import pallas as pl
from jax.experimental.pallas import tpu as pltpu
from jax.sharding import PartitionSpec as P

HEADS = 8
DK = 128
TILE = 256
F32 = jnp.float32
BF16 = jnp.bfloat16
MESH = pl.DeviceIdType.MESH


def pieces_of(dp, rows):
    for g in (4, 2):
        if dp % g == 0 and rows % (16 * g) == 0:
            return g
    return 1


def kernel(
    cfg, x_hbm, cgain, cw_hbm, cbias, again, q_hbm, kv_hbm, o_hbm, cs_ref,
    skip_hbm, out_hbm,
    xin, halo, resid, pad, stack, cw, acc, skip, normed, wq, wkv, wo, own, kvbuf, queries,
    peak, attn, mixed, outv,
    in_sem, cw_sem, loc_sem, halo_s, halo_r, p1_s, p1_r, p2_s, p2_r, p3_s, p3_r, p4_s, p4_r,
    kd_s, kd_r, kp_s, kp_r, out_sem,
):
    D, S, G, R = cfg
    Z = S // 2
    rows, width = xin.shape
    toks = rows // 2
    n_tiles = width // TILE
    taps = cw.shape[1]
    dv = kv_hbm.shape[1] - DK
    d = lax.axis_index("dp")
    s = lax.axis_index("seq")
    c = lax.rem(s, 2)
    z = s // 2
    partner = s + 1 - 2 * c
    rp = R // G
    me = d % G
    if G == 4:
        f1 = d + 1 - 2 * (d % 2)
        f2 = d + 2 - 4 * ((d // 2) % 2)
        ax1 = f1 + c * (f2 - f1)
        ax2 = f2 + c * (f1 - f2)
    elif G == 2:
        ax1 = d + 1 - 2 * (d % 2)
        ax2 = None
    else:
        ax1 = ax2 = None

    up = (s + 1) % S
    down = (s + S - 1) % S

    def fwd(k):
        return ((z + k) % Z) * 2 + c

    def src(k):
        return ((z + Z - k) % Z) * 2 + c

    in_copy = pltpu.make_async_copy(x_hbm, xin, in_sem)
    in_copy.start()
    cw_copies = []
    for n in range(n_tiles):
        cp = pltpu.make_async_copy(
            cw_hbm.at[:, :, pl.ds(n * TILE, TILE)], cw.at[n], cw_sem.at[n]
        )
        cp.start()
        cw_copies.append(cp)

    greet = [(d, up), (d, down), (d, partner)] + [(d, fwd(k)) for k in range(1, Z)]
    if ax1 is not None:
        greet.append((ax1, s))
    if ax2 is not None:
        greet.append((ax2, s))
    bar = pltpu.get_barrier_semaphore()
    for g in greet:
        pl.semaphore_signal(bar, inc=1, device_id=g, device_id_type=MESH)
    pl.semaphore_wait(bar, len(greet))

    def remote(a, b, ss, rs, dev):
        return pltpu.make_async_remote_copy(
            src_ref=a, dst_ref=b, send_sem=ss, recv_sem=rs, device_id=dev, device_id_type=MESH
        )

    sent = []

    def start(cp):
        cp.start()
        sent.append(cp)
        return cp

    h_up = start(remote(x_hbm.at[pl.ds(rows - 16, 16)], halo.at[0], halo_s.at[0], halo_r.at[0], (d, up)))
    h_dn = start(remote(x_hbm.at[pl.ds(0, 16)], halo.at[1], halo_s.at[1], halo_r.at[1], (d, down)))

    hbms = (kv_hbm, q_hbm, o_hbm)
    bufs = (wkv, wq, wo)

    def al(v, m):
        return pl.multiple_of(v, m)

    ph1, ph2, ph3, ph4, locs = {}, {}, {}, {}, {}

    def phase1(a):
        for k in range(1, Z):
            at = pl.ds(al(me * rp, 16), rp)
            to = pl.ds(al(s * R + me * rp, 16), rp)
            ph1[a, k] = start(remote(
                hbms[a].at[at], bufs[a].at[to], p1_s.at[a, k - 1], p1_r.at[a, k - 1], (d, fwd(k))
            ))
        whole = pl.ds(al(s * R, 16), R)
        ph4[a, 0] = start(remote(
            hbms[a], bufs[a].at[whole], p4_s.at[a, 0], p4_r.at[a, 0], (d, partner)
        ))
        locs[a] = pltpu.make_async_copy(hbms[a], bufs[a].at[whole], loc_sem.at[a])
        locs[a].start()

    def phase2(a):
        for k in range(1, Z):
            ph1[a, k].wait_recv()
            if ax1 is not None:
                at = bufs[a].at[pl.ds(al(src(k) * R + me * rp, 16), rp)]
                ph2[a, k] = start(remote(at, at, p2_s.at[a, k - 1], p2_r.at[a, k - 1], (ax1, s)))

    def phase3(a):
        for k in range(1, Z):
            if ax1 is not None:
                ph2[a, k].wait_recv()
            if ax2 is not None:
                for i, piece in enumerate((me, ax1 % G)):
                    at = bufs[a].at[pl.ds(al(src(k) * R + piece * rp, 16), rp)]
                    ph3[a, k, i] = start(remote(
                        at, at, p3_s.at[a, k - 1, i], p3_r.at[a, k - 1, i], (ax2, s)
                    ))

    def phase4(a):
        for k in range(1, Z):
            if ax2 is not None:
                ph3[a, k, 0].wait_recv()
                ph3[a, k, 1].wait_recv()
            at = bufs[a].at[pl.ds(al(src(k) * R, 16), R)]
            ph4[a, k] = start(remote(at, at, p4_s.at[a, k], p4_r.at[a, k], (d, partner)))

    def ready(a):
        locs[a].wait()
        for k in range(Z):
            ph4[a, k].wait_recv()

    phase1(0)
    phase1(1)

    def act(v):
        scale = lax.rsqrt(jnp.mean(v * v, axis=-1, keepdims=True) + 1e-06)
        return jax.nn.gelu(v * scale * cgain[...], approximate=True)

    in_copy.wait()
    step_rows = 16

    def act_rows(i, carry):
        at = al(i * step_rows, step_rows)
        v = xin[pl.ds(at, step_rows), :].astype(F32)
        a = act(v)
        for j in range(width // 128):
            resid[j, pl.ds(at, step_rows), :] = v[:, j * 128:(j + 1) * 128]
            pad[j, pl.ds(al(8 + i * step_rows, 8), step_rows), :] = a[:, j * 128:(j + 1) * 128]
        return carry

    lax.fori_loop(0, rows // step_rows, act_rows, 0)
    h_up.wait_recv()
    h_dn.wait_recv()
    before = act(halo[0].astype(F32))[8:16, :] * jnp.where(s > 0, 1.0, 0.0).astype(F32)
    after = act(halo[1].astype(F32))[0:8, :] * jnp.where(s < S - 1, 1.0, 0.0).astype(F32)
    for j in range(width // 128):
        cols = slice(j * 128, (j + 1) * 128)
        pad[j, 0:8, :] = before[:, cols]
        pad[j, rows + 8:rows + 16, :] = after[:, cols]
        for b in range(taps + 1):
            stack[b * toks:(b + 1) * toks, cols] = pad[
                j, pl.ds(6 + b, toks, stride=2), :
            ].astype(BF16)

    events = {1: (lambda: phase2(0), lambda: phase2(1), lambda: phase1(2)),
              3: (lambda: phase3(0), lambda: phase3(1)),
              4: (lambda: phase4(0), lambda: phase4(1))}
    for n in range(n_tiles):
        cw_copies[n].wait()
        acc[...] = jnp.broadcast_to(cbias[:, n * TILE:(n + 1) * TILE], acc.shape)

        def tap(t, carry):
            acc[...] += jnp.dot(
                stack[pl.ds(al(t * toks, 16), 2 * toks), :], cw[n, t], preferred_element_type=F32
            )
            return carry

        lax.fori_loop(0, taps, tap, 0)
        for i in range(TILE // 128):
            j = n * TILE // 128 + i
            part = slice(i * 128, (i + 1) * 128)
            even = resid[j, pl.ds(0, toks, stride=2), :] + acc[0:toks, part]
            odd = resid[j, pl.ds(1, toks, stride=2), :] + acc[toks:2 * toks, part]
            skip[:, j * 128:(j + 1) * 128] = jnp.maximum(even, odd).astype(BF16)
        for e in events.get(n, ()):
            e()

    skip_out = pltpu.make_async_copy(skip, skip_hbm, out_sem.at[0])
    skip_out.start()

    def norm_rows(i, carry):
        at = pl.ds(al(i * 16, 16), 16)
        v = skip[at, :].astype(F32)
        scale = lax.rsqrt(jnp.mean(v * v, axis=-1, keepdims=True) + 1e-06)
        normed[at, :] = (v * scale * again[...]).astype(BF16)
        return carry

    lax.fori_loop(0, toks // 16, norm_rows, 0)

    cosine = cs_ref[:, 0:DK]
    sine = cs_ref[:, DK:2 * DK]

    def rotate(v):
        return v * cosine + pltpu.roll(v, DK // 2, 1) * sine

    ready(0)
    projected = jnp.dot(normed[...], wkv[...], preferred_element_type=F32)
    own[:, 0:DK] = rotate(projected[:, 0:DK]).astype(BF16)
    lanes = own.shape[1] - DK - dv
    own[:, DK:DK + dv] = projected[:, DK:].astype(BF16)
    own[:, DK + dv:] = jnp.ones((toks, lanes), BF16)
    mine = kvbuf.at[pl.ds(al(s * toks, 16), toks)]
    own_copy = pltpu.make_async_copy(own, mine, loc_sem.at[3])
    own_copy.start()
    own_copy.wait()
    kp = {0: start(remote(mine, mine, kp_s.at[0], kp_r.at[0], (d, partner)))}
    kd = {}
    for k in range(1, Z):
        kd[k] = start(remote(mine, mine, kd_s.at[k - 1], kd_r.at[k - 1], (d, fwd(k))))

    ready(1)
    for h in range(HEADS // 2):
        both = jnp.dot(
            normed[...], wq[:, 2 * h * DK:(2 * h + 2) * DK], preferred_element_type=F32
        )
        queries[2 * h] = rotate(both[:, 0:DK]).astype(BF16)
        queries[2 * h + 1] = rotate(both[:, DK:]).astype(BF16)
    phase2(2)

    factor = DK ** (-0.5) * 1.4426950408889634
    for k in range(Z):
        if k > 0:
            kd[k].wait_recv()
            theirs = kvbuf.at[pl.ds(al(src(k) * toks, 16), toks)]
            kp[k] = start(remote(theirs, theirs, kp_s.at[k], kp_r.at[k], (d, partner)))
        kp[k].wait_recv()
        first = k == 0
        base = al(((z + Z - k) % Z) * 2 * toks, 16)

        def head(h, carry):
            keys = kvbuf[pl.ds(base, 2 * toks), 0:DK]
            values = kvbuf[pl.ds(base, 2 * toks), DK:]
            scores = lax.dot_general(
                queries[h], keys, (((1,), (1,)), ((), ())), preferred_element_type=F32
            )
            top = jnp.max(scores, axis=-1, keepdims=True)
            if not first:
                old = peak[h][:, 0:1]
                top = jnp.maximum(old, top)
            weights = jnp.exp2((scores - top) * factor).astype(BF16)
            got = jnp.dot(weights, values, preferred_element_type=F32)
            if not first:
                got = got + attn[h] * jnp.exp2((old - top) * factor)
            attn[h] = got
            peak[h] = jnp.broadcast_to(top, (toks, 128))
            return carry

        lax.fori_loop(0, HEADS, head, 0)
        if k == 0:
            phase3(2)
        if k == 1:
            phase4(2)

    for h in range(HEADS):
        a = attn[h]
        mixed[:, h * dv:(h + 1) * dv] = (a[:, 0:dv] / a[:, dv:dv + 1]).astype(BF16)

    ready(2)

    outs = []
    for n in range(n_tiles):
        cols = slice(n * TILE, (n + 1) * TILE)
        got = jnp.dot(mixed[...], wo[:, cols], preferred_element_type=F32)
        outv[:, cols] = (skip[:, cols].astype(F32) + got).astype(BF16)
    out_copy = pltpu.make_async_copy(outv, out_hbm, out_sem.at[1])
    out_copy.start()
    for cp in sent:
        cp.wait_send()
    skip_out.wait()
    out_copy.wait()


def body(mesh, section_input, conv_gain, conv_weight, conv_bias, attn_gain, q_weight, kv_weight, o_weight):
    D, S = mesh.shape["dp"], mesh.shape["seq"]
    Z = S // 2
    rows, width = section_input.shape
    toks = rows // 2
    R = q_weight.shape[0]
    G = pieces_of(D, R)
    taps = conv_weight.shape[0]
    nq, nkv, hv = q_weight.shape[1], kv_weight.shape[1], R * S
    dv = nkv - DK
    positions = lax.axis_index("seq") * toks + jnp.arange(toks, dtype=jnp.int32)
    half = DK // 2
    freqs = jnp.power(10000.0, -jnp.arange(half, dtype=F32) / half)
    angle = positions.astype(F32)[:, None] * freqs[None, :]
    co, si = jnp.cos(angle), jnp.sin(angle)
    cs = jnp.concatenate([co, co, -si, si], axis=-1)
    anys = pl.BlockSpec(memory_space=pl.ANY)
    vmem = pl.BlockSpec(memory_space=pltpu.VMEM)
    dma = pltpu.SemaphoreType.DMA
    lanes = -(-nkv // 128) * 128
    if lanes == nkv:
        lanes += 128
    z1 = max(Z - 1, 1)
    return pl.pallas_call(
        functools.partial(kernel, (D, S, G, R)),
        out_shape=(
            jax.ShapeDtypeStruct((toks, width), BF16),
            jax.ShapeDtypeStruct((toks, width), BF16),
        ),
        in_specs=[anys, vmem, anys, vmem, vmem, anys, anys, anys, vmem],
        out_specs=(anys, anys),
        scratch_shapes=[
            pltpu.VMEM((rows, width), BF16),
            pltpu.VMEM((2, 16, width), BF16),
            pltpu.VMEM((width // 128, rows, 128), F32),
            pltpu.VMEM((width // 128, rows + 16, 128), F32),
            pltpu.VMEM(((taps + 1) * toks, width), BF16),
            pltpu.VMEM((width // TILE, taps, width, TILE), BF16),
            pltpu.VMEM((rows, TILE), F32),
            pltpu.VMEM((toks, width), BF16),
            pltpu.VMEM((toks, width), BF16),
            pltpu.VMEM((R * S, nq), BF16),
            pltpu.VMEM((R * S, nkv), BF16),
            pltpu.VMEM((R * S, width), BF16),
            pltpu.VMEM((toks, lanes), BF16),
            pltpu.VMEM((S * toks, lanes), BF16),
            pltpu.VMEM((HEADS, toks, DK), BF16),
            pltpu.VMEM((HEADS, toks, 128), F32),
            pltpu.VMEM((HEADS, toks, lanes - DK), F32),
            pltpu.VMEM((toks, hv), BF16),
            pltpu.VMEM((toks, width), BF16),
            dma, dma((width // TILE,)), dma((4,)),
            dma((2,)), dma((2,)),
            dma((3, z1)), dma((3, z1)), dma((3, z1)), dma((3, z1)),
            dma((3, z1, 2)), dma((3, z1, 2)), dma((3, Z)), dma((3, Z)),
            dma((z1,)), dma((z1,)), dma((Z,)), dma((Z,)), dma((2,)),
        ],
        compiler_params=pltpu.CompilerParams(
            collective_id=0, has_side_effects=True, vmem_limit_bytes=66 * 1000 * 1000
        ),
        name="block",
    )(
        section_input, conv_gain[None, :], conv_weight, conv_bias[None, :], attn_gain[None, :],
        q_weight, kv_weight, o_weight, cs,
    )


def solution(mesh):
    row = P(("dp", "seq"), None)
    seq = P("seq", None)
    in_specs = (row, P(), P(), P(), P(), seq, seq, seq)
    return jax.shard_map(
        functools.partial(body, mesh), mesh=mesh, in_specs=in_specs, out_specs=(row, row), check_vma=False
    )
```

```python
import functools

import jax
import jax.numpy as jnp
from jax import lax
from jax.experimental import pallas as pl
from jax.experimental.pallas import tpu as pltpu
from jax.sharding import PartitionSpec as P

HEADS = 8
DK = 128
TILE = 256
UNROLL = 4
F32 = jnp.float32
BF16 = jnp.bfloat16
MESH = pl.DeviceIdType.MESH


def pieces_of(dp, rows):
    for g in (4, 2):
        if dp % g == 0 and rows % (16 * g) == 0:
            return g
    return 1


def kernel(
    cfg, x_hbm, cgain, cw_hbm, cbias, again, q_hbm, kv_hbm, o_hbm, cos_ref, sin_ref,
    skip_hbm, out_hbm,
    xin, halo, resid, pad, stack, cw, acc, skip, normed, wq, wkv, wo, own_k, own_v, kbuf, vbuf, queries,
    peak, attn, mixed, outv, vecs,
    in_sem, cw_sem, loc_sem, halo_s, halo_r, p1_s, p1_r, p2_s, p2_r, p3_s, p3_r, p4_s, p4_r,
    kd_s, kd_r, kp_s, kp_r, out_sem,
):
    D, S, G, R = cfg
    Z = S // 2
    rows, width = xin.shape
    toks = rows // 2
    n_tiles = width // TILE
    taps = cw.shape[1]
    dv = kv_hbm.shape[1] - DK
    d = lax.axis_index("dp")
    s = lax.axis_index("seq")
    c = lax.rem(s, 2)
    z = s // 2
    partner = s + 1 - 2 * c
    rp = R // G
    me = d % G
    if G == 4:
        f1 = d + 1 - 2 * (d % 2)
        f2 = d + 2 - 4 * ((d // 2) % 2)
        ax1 = f1 + c * (f2 - f1)
        ax2 = f2 + c * (f1 - f2)
    elif G == 2:
        ax1 = d + 1 - 2 * (d % 2)
        ax2 = None
    else:
        ax1 = ax2 = None

    up = (s + 1) % S
    down = (s + S - 1) % S

    def fwd(k):
        return ((z + k) % Z) * 2 + c

    def src(k):
        return ((z + Z - k) % Z) * 2 + c

    in_copy = pltpu.make_async_copy(x_hbm, xin, in_sem)
    in_copy.start()
    cw_copies = []
    for n in range(n_tiles):
        cp = pltpu.make_async_copy(
            cw_hbm.at[:, :, pl.ds(n * TILE, TILE)], cw.at[n], cw_sem.at[n]
        )
        cp.start()
        cw_copies.append(cp)

    greet = [(d, up), (d, down), (d, partner)] + [(d, fwd(k)) for k in range(1, Z)]
    if ax1 is not None:
        greet.append((ax1, s))
    if ax2 is not None:
        greet.append((ax2, s))
    bar = pltpu.get_barrier_semaphore()
    for g in greet:
        pl.semaphore_signal(bar, inc=1, device_id=g, device_id_type=MESH)
    pl.semaphore_wait(bar, len(greet))

    def remote(a, b, ss, rs, dev):
        return pltpu.make_async_remote_copy(
            src_ref=a, dst_ref=b, send_sem=ss, recv_sem=rs, device_id=dev, device_id_type=MESH
        )

    sent = []

    def start(cp):
        cp.start()
        sent.append(cp)
        return cp

    h_up = start(remote(x_hbm.at[pl.ds(rows - 16, 16)], halo.at[0], halo_s.at[0], halo_r.at[0], (d, up)))
    h_dn = start(remote(x_hbm.at[pl.ds(0, 16)], halo.at[1], halo_s.at[1], halo_r.at[1], (d, down)))

    hbms = (kv_hbm, q_hbm, o_hbm)
    bufs = (wkv, wq, wo)

    def al(v, m):
        return pl.multiple_of(v, m)

    ph1, ph2, ph3, ph4, locs = {}, {}, {}, {}, {}

    def phase1(a):
        for k in range(1, Z):
            at = pl.ds(al(me * rp, 16), rp)
            to = pl.ds(al(s * R + me * rp, 16), rp)
            ph1[a, k] = start(remote(
                hbms[a].at[at], bufs[a].at[to], p1_s.at[a, k - 1], p1_r.at[a, k - 1], (d, fwd(k))
            ))
        whole = pl.ds(al(s * R, 16), R)
        ph4[a, 0] = start(remote(
            hbms[a], bufs[a].at[whole], p4_s.at[a, 0], p4_r.at[a, 0], (d, partner)
        ))
        locs[a] = pltpu.make_async_copy(hbms[a], bufs[a].at[whole], loc_sem.at[a])
        locs[a].start()

    def phase2(a):
        for k in range(1, Z):
            ph1[a, k].wait_recv()
            if ax1 is not None:
                at = bufs[a].at[pl.ds(al(src(k) * R + me * rp, 16), rp)]
                ph2[a, k] = start(remote(at, at, p2_s.at[a, k - 1], p2_r.at[a, k - 1], (ax1, s)))

    def phase3(a):
        for k in range(1, Z):
            if ax1 is not None:
                ph2[a, k].wait_recv()
            if ax2 is not None:
                for i, piece in enumerate((me, ax1 % G)):
                    at = bufs[a].at[pl.ds(al(src(k) * R + piece * rp, 16), rp)]
                    ph3[a, k, i] = start(remote(
                        at, at, p3_s.at[a, k - 1, i], p3_r.at[a, k - 1, i], (ax2, s)
                    ))

    def phase4(a):
        for k in range(1, Z):
            if ax2 is not None:
                ph3[a, k, 0].wait_recv()
                ph3[a, k, 1].wait_recv()
            at = bufs[a].at[pl.ds(al(src(k) * R, 16), R)]
            ph4[a, k] = start(remote(at, at, p4_s.at[a, k], p4_r.at[a, k], (d, partner)))

    def ready(a):
        locs[a].wait()
        for k in range(Z):
            ph4[a, k].wait_recv()

    phase1(0)
    phase1(1)

    for i, vec in enumerate((cgain, cbias, again)):
        vecs[i:i + 1, :] = vec[...].reshape(1, width)

    def act(v):
        scale = lax.rsqrt(jnp.mean(v * v, axis=-1, keepdims=True) + 1e-06)
        return jax.nn.gelu(v * scale * vecs[0:1, :], approximate=True)

    in_copy.wait()
    step_rows = 16

    def act_rows(i, carry):
        at = al(i * step_rows, step_rows)
        v = xin[pl.ds(at, step_rows), :].astype(F32)
        a = act(v)
        for j in range(width // 128):
            resid[j, pl.ds(at, step_rows), :] = v[:, j * 128:(j + 1) * 128]
            pad[j, pl.ds(al(8 + i * step_rows, 8), step_rows), :] = a[:, j * 128:(j + 1) * 128]
        return carry

    lax.fori_loop(0, rows // step_rows, act_rows, 0)
    h_up.wait_recv()
    h_dn.wait_recv()
    before = act(halo[0].astype(F32))[8:16, :] * jnp.where(s > 0, 1.0, 0.0).astype(F32)
    after = act(halo[1].astype(F32))[0:8, :] * jnp.where(s < S - 1, 1.0, 0.0).astype(F32)
    for j in range(width // 128):
        cols = slice(j * 128, (j + 1) * 128)
        pad[j, 0:8, :] = before[:, cols]
        pad[j, rows + 8:rows + 16, :] = after[:, cols]
        for b in range(taps + 1):
            stack[b * toks:(b + 1) * toks, cols] = pad[
                j, pl.ds(6 + b, toks, stride=2), :
            ].astype(BF16)

    events = {1: (lambda: phase2(0), lambda: phase2(1), lambda: phase1(2)),
              3: (lambda: phase3(0), lambda: phase3(1)),
              4: (lambda: phase4(0), lambda: phase4(1))}
    for n in range(n_tiles):
        cw_copies[n].wait()
        acc[...] = jnp.broadcast_to(vecs[1:2, n * TILE:(n + 1) * TILE], acc.shape)

        def tap(t, carry):
            acc[...] += jnp.dot(
                stack[pl.ds(al(t * toks, 16), 2 * toks), :], cw[n, t], preferred_element_type=F32
            )
            return carry

        lax.fori_loop(0, taps, tap, 0)
        for i in range(TILE // 128):
            j = n * TILE // 128 + i
            part = slice(i * 128, (i + 1) * 128)
            even = resid[j, pl.ds(0, toks, stride=2), :] + acc[0:toks, part]
            odd = resid[j, pl.ds(1, toks, stride=2), :] + acc[toks:2 * toks, part]
            skip[:, j * 128:(j + 1) * 128] = jnp.maximum(even, odd).astype(BF16)
        for e in events.get(n, ()):
            e()

    skip_out = pltpu.make_async_copy(skip, skip_hbm, out_sem.at[0])
    skip_out.start()

    def norm_rows(i, carry):
        at = pl.ds(al(i * 16, 16), 16)
        v = skip[at, :].astype(F32)
        scale = lax.rsqrt(jnp.mean(v * v, axis=-1, keepdims=True) + 1e-06)
        normed[at, :] = (v * scale * vecs[2:3, :]).astype(BF16)
        return carry

    lax.fori_loop(0, toks // 16, norm_rows, 0)

    cosine = cos_ref[...]
    sine = sin_ref[...]

    def rotate(v):
        return v * cosine + pltpu.roll(v, DK // 2, 1) * sine

    ready(0)
    projected = jnp.dot(normed[...], wkv[...], preferred_element_type=F32)
    own_k[...] = rotate(projected[:, 0:DK]).astype(BF16)
    own_v[0:dv, :] = jnp.transpose(projected[:, DK:]).astype(BF16)
    own_v[dv:, :] = jnp.ones((own_v.shape[0] - dv, toks), BF16)
    mine = (kbuf.at[s], vbuf.at[s])
    own_copies = []
    for i, (a, b) in enumerate(zip((own_k, own_v), mine)):
        cp = pltpu.make_async_copy(a, b, loc_sem.at[3 + i])
        cp.start()
        own_copies.append(cp)
    for cp in own_copies:
        cp.wait()
    kp, kd = {}, {}
    for i, a in enumerate(mine):
        kp[0, i] = start(remote(a, a, kp_s.at[i, 0], kp_r.at[i, 0], (d, partner)))
    for k in range(1, Z):
        for i, a in enumerate(mine):
            kd[k, i] = start(remote(a, a, kd_s.at[i, k - 1], kd_r.at[i, k - 1], (d, fwd(k))))

    ready(1)
    for h in range(HEADS // 2):
        both = jnp.dot(
            normed[...], wq[:, 2 * h * DK:(2 * h + 2) * DK], preferred_element_type=F32
        )
        queries[2 * h] = rotate(both[:, 0:DK]).astype(BF16)
        queries[2 * h + 1] = rotate(both[:, DK:]).astype(BF16)
    phase2(2)

    factor = DK ** (-0.5) * 1.4426950408889634
    for k in range(Z):
        for i, buf in enumerate((kbuf, vbuf)):
            if k > 0:
                kd[k, i].wait_recv()
                at = buf.at[src(k)]
                kp[k, i] = start(remote(at, at, kp_s.at[i, k], kp_r.at[i, k], (d, partner)))
        for i in range(2):
            kp[k, i].wait_recv()
        first = k == 0
        base = ((z + Z - k) % Z) * 2

        def head(h):
            scores = [
                lax.dot_general(
                    kbuf[base + j], queries[h], (((1,), (1,)), ((), ())), preferred_element_type=F32
                )
                for j in range(2)
            ]
            top = jnp.max(jnp.maximum(scores[0], scores[1]), axis=0, keepdims=True)
            if not first:
                old = peak[h][0:1, :]
                top = jnp.maximum(old, top)
            got = None
            for j in range(2):
                weights = jnp.exp2((scores[j] - top) * factor).astype(BF16)
                part = jnp.dot(vbuf[base + j], weights, preferred_element_type=F32)
                got = part if got is None else got + part
            if not first:
                got = got + attn[h] * jnp.exp2((old - top) * factor)
            attn[h] = got
            peak[h] = jnp.broadcast_to(top, (8, toks))

        def heads(i, carry):
            for u in range(UNROLL):
                head(i * UNROLL + u)
            return carry

        lax.fori_loop(0, HEADS // UNROLL, heads, 0)
        if k == 0:
            phase3(2)
        if k == 1:
            phase4(2)

    for h in range(HEADS):
        a = attn[h]
        mixed[:, h * dv:(h + 1) * dv] = jnp.transpose(a[0:dv, :] / a[dv:dv + 1, :]).astype(BF16)

    ready(2)

    outs = []
    for n in range(n_tiles):
        cols = slice(n * TILE, (n + 1) * TILE)
        got = jnp.dot(mixed[...], wo[:, cols], preferred_element_type=F32)
        outv[:, cols] = (skip[:, cols].astype(F32) + got).astype(BF16)
    out_copy = pltpu.make_async_copy(outv, out_hbm, out_sem.at[1])
    out_copy.start()
    for cp in sent:
        cp.wait_send()
    skip_out.wait()
    out_copy.wait()


def body(mesh, section_input, conv_gain, conv_weight, conv_bias, attn_gain, q_weight, kv_weight, o_weight):
    D, S = mesh.shape["dp"], mesh.shape["seq"]
    Z = S // 2
    rows, width = section_input.shape
    toks = rows // 2
    R = q_weight.shape[0]
    G = pieces_of(D, R)
    taps = conv_weight.shape[0]
    nq, nkv, hv = q_weight.shape[1], kv_weight.shape[1], R * S
    dv = nkv - DK
    positions = lax.axis_index("seq") * toks + jnp.arange(toks, dtype=jnp.int32)
    half = DK // 2
    freqs = jnp.power(10000.0, -(jnp.arange(DK, dtype=jnp.int32) % half).astype(F32) / half)
    angle = positions.astype(F32)[:, None] * freqs[None, :]
    cosine = jnp.cos(angle)
    sine = jnp.sin(angle) * jnp.where(jnp.arange(DK) < half, -1.0, 1.0).astype(F32)
    anys = pl.BlockSpec(memory_space=pl.ANY)
    vmem = pl.BlockSpec(memory_space=pltpu.VMEM)
    dma = pltpu.SemaphoreType.DMA
    z1 = max(Z - 1, 1)
    return pl.pallas_call(
        functools.partial(kernel, (D, S, G, R)),
        out_shape=(
            jax.ShapeDtypeStruct((toks, width), BF16),
            jax.ShapeDtypeStruct((toks, width), BF16),
        ),
        in_specs=[anys, vmem, anys, vmem, vmem, anys, anys, anys, vmem, vmem],
        out_specs=(anys, anys),
        scratch_shapes=[
            pltpu.VMEM((rows, width), BF16),
            pltpu.VMEM((2, 16, width), BF16),
            pltpu.VMEM((width // 128, rows, 128), F32),
            pltpu.VMEM((width // 128, rows + 16, 128), F32),
            pltpu.VMEM(((taps + 1) * toks, width), BF16),
            pltpu.VMEM((width // TILE, taps, width, TILE), BF16),
            pltpu.VMEM((rows, TILE), F32),
            pltpu.VMEM((toks, width), BF16),
            pltpu.VMEM((toks, width), BF16),
            pltpu.VMEM((R * S, nq), BF16),
            pltpu.VMEM((R * S, nkv), BF16),
            pltpu.VMEM((R * S, width), BF16),
            pltpu.VMEM((toks, DK), BF16),
            pltpu.VMEM((dv + 16, toks), BF16),
            pltpu.VMEM((S, toks, DK), BF16),
            pltpu.VMEM((S, dv + 16, toks), BF16),
            pltpu.VMEM((HEADS, toks, DK), BF16),
            pltpu.VMEM((HEADS, 8, toks), F32),
            pltpu.VMEM((HEADS, dv + 16, toks), F32),
            pltpu.VMEM((toks, hv), BF16),
            pltpu.VMEM((toks, width), BF16),
            pltpu.VMEM((8, width), F32),
            dma, dma((width // TILE,)), dma((5,)),
            dma((2,)), dma((2,)),
            dma((3, z1)), dma((3, z1)), dma((3, z1)), dma((3, z1)),
            dma((3, z1, 2)), dma((3, z1, 2)), dma((3, Z)), dma((3, Z)),
            dma((2, z1)), dma((2, z1)), dma((2, Z)), dma((2, Z)), dma((2,)),
        ],
        compiler_params=pltpu.CompilerParams(
            collective_id=0, vmem_limit_bytes=66 * 1000 * 1000
        ),
        name="block",
    )(
        section_input, conv_gain, conv_weight, conv_bias, attn_gain, q_weight, kv_weight, o_weight,
        cosine, sine,
    )


def solution(mesh):
    row = P(("dp", "seq"), None)
    seq = P("seq", None)
    in_specs = (row, P(), P(), P(), P(), seq, seq, seq)
    return jax.shard_map(
        functools.partial(body, mesh), mesh=mesh, in_specs=in_specs, out_specs=(row, row), check_vma=False
    )
```

```python
import functools

import jax
import jax.numpy as jnp
from jax import lax
from jax.experimental import pallas as pl
from jax.experimental.pallas import tpu as pltpu
from jax.sharding import PartitionSpec as P

HEADS = 8
DK = 128
TILE = 256
UNROLL = 4
F32 = jnp.float32
BF16 = jnp.bfloat16
MESH = pl.DeviceIdType.MESH


def pieces_of(dp, rows):
    for g in (4, 2):
        if dp % g == 0 and rows % (16 * g) == 0:
            return g
    return 1


def kernel(
    cfg, x_hbm, cgain, cw_hbm, cbias, again, q_hbm, kv_hbm, o_hbm, cos_ref, sin_ref,
    skip, outv,
    xin, halo, resid, pad, stack, cw, acc, normed, wq, wkv, wo, own_k, own_v, kbuf, vbuf, queries,
    peak, attn, mixed, vecs,
    in_sem, cw_sem, loc_sem, halo_s, halo_r, p1_s, p1_r, p2_s, p2_r, p3_s, p3_r, p4_s, p4_r,
    kd_s, kd_r, kp_s, kp_r,
):
    D, S, G, R = cfg
    Z = S // 2
    rows, width = xin.shape
    toks = rows // 2
    n_tiles = width // TILE
    taps = cw.shape[1]
    dv = kv_hbm.shape[1] - DK
    d = lax.axis_index("dp")
    s = lax.axis_index("seq")
    c = lax.rem(s, 2)
    z = s // 2
    partner = s + 1 - 2 * c
    rp = R // G
    me = d % G
    if G == 4:
        f1 = d + 1 - 2 * (d % 2)
        f2 = d + 2 - 4 * ((d // 2) % 2)
        ax1 = f1 + c * (f2 - f1)
        ax2 = f2 + c * (f1 - f2)
    elif G == 2:
        ax1 = d + 1 - 2 * (d % 2)
        ax2 = None
    else:
        ax1 = ax2 = None

    up = (s + 1) % S
    down = (s + S - 1) % S

    def fwd(k):
        return ((z + k) % Z) * 2 + c

    def src(k):
        return ((z + Z - k) % Z) * 2 + c

    in_copy = pltpu.make_async_copy(x_hbm, xin, in_sem)
    in_copy.start()
    cw_copies = []
    for n in range(n_tiles):
        cp = pltpu.make_async_copy(
            cw_hbm.at[:, :, pl.ds(n * TILE, TILE)], cw.at[n], cw_sem.at[n]
        )
        cp.start()
        cw_copies.append(cp)

    greet = [(d, up), (d, down), (d, partner)] + [(d, fwd(k)) for k in range(1, Z)]
    if ax1 is not None:
        greet.append((ax1, s))
    if ax2 is not None:
        greet.append((ax2, s))
    bar = pltpu.get_barrier_semaphore()
    for g in greet:
        pl.semaphore_signal(bar, inc=1, device_id=g, device_id_type=MESH)
    pl.semaphore_wait(bar, len(greet))

    def remote(a, b, ss, rs, dev):
        return pltpu.make_async_remote_copy(
            src_ref=a, dst_ref=b, send_sem=ss, recv_sem=rs, device_id=dev, device_id_type=MESH
        )

    sent = []

    def start(cp):
        cp.start()
        sent.append(cp)
        return cp

    h_up = start(remote(x_hbm.at[pl.ds(rows - 16, 16)], halo.at[0], halo_s.at[0], halo_r.at[0], (d, up)))
    h_dn = start(remote(x_hbm.at[pl.ds(0, 16)], halo.at[1], halo_s.at[1], halo_r.at[1], (d, down)))

    hbms = (kv_hbm, q_hbm, o_hbm)
    bufs = (wkv, wq, wo)

    def al(v, m):
        return pl.multiple_of(v, m)

    ph1, ph2, ph3, ph4, locs = {}, {}, {}, {}, {}

    def phase1(a):
        for k in range(1, Z):
            at = pl.ds(al(me * rp, 16), rp)
            to = pl.ds(al(s * R + me * rp, 16), rp)
            ph1[a, k] = start(remote(
                hbms[a].at[at], bufs[a].at[to], p1_s.at[a, k - 1], p1_r.at[a, k - 1], (d, fwd(k))
            ))
        whole = pl.ds(al(s * R, 16), R)
        ph4[a, 0] = start(remote(
            hbms[a], bufs[a].at[whole], p4_s.at[a, 0], p4_r.at[a, 0], (d, partner)
        ))
        locs[a] = pltpu.make_async_copy(hbms[a], bufs[a].at[whole], loc_sem.at[a])
        locs[a].start()

    def phase2(a):
        for k in range(1, Z):
            ph1[a, k].wait_recv()
            if ax1 is not None:
                at = bufs[a].at[pl.ds(al(src(k) * R + me * rp, 16), rp)]
                ph2[a, k] = start(remote(at, at, p2_s.at[a, k - 1], p2_r.at[a, k - 1], (ax1, s)))

    def phase3(a):
        for k in range(1, Z):
            if ax1 is not None:
                ph2[a, k].wait_recv()
            if ax2 is not None:
                for i, piece in enumerate((me, ax1 % G)):
                    at = bufs[a].at[pl.ds(al(src(k) * R + piece * rp, 16), rp)]
                    ph3[a, k, i] = start(remote(
                        at, at, p3_s.at[a, k - 1, i], p3_r.at[a, k - 1, i], (ax2, s)
                    ))

    def phase4(a):
        for k in range(1, Z):
            if ax2 is not None:
                ph3[a, k, 0].wait_recv()
                ph3[a, k, 1].wait_recv()
            at = bufs[a].at[pl.ds(al(src(k) * R, 16), R)]
            ph4[a, k] = start(remote(at, at, p4_s.at[a, k], p4_r.at[a, k], (d, partner)))

    def ready(a):
        locs[a].wait()
        for k in range(Z):
            ph4[a, k].wait_recv()

    phase1(0)
    phase1(1)

    for i, vec in enumerate((cgain, cbias, again)):
        vecs[i:i + 1, :] = vec[...].reshape(1, width)

    def act(v):
        scale = lax.rsqrt(jnp.mean(v * v, axis=-1, keepdims=True) + 1e-06)
        return jax.nn.gelu(v * scale * vecs[0:1, :], approximate=True)

    in_copy.wait()
    step_rows = 16

    def act_rows(i, carry):
        at = al(i * step_rows, step_rows)
        v = xin[pl.ds(at, step_rows), :].astype(F32)
        a = act(v)
        for j in range(width // 128):
            resid[j, pl.ds(at, step_rows), :] = v[:, j * 128:(j + 1) * 128]
            pad[j, pl.ds(al(8 + i * step_rows, 8), step_rows), :] = a[:, j * 128:(j + 1) * 128]
        return carry

    lax.fori_loop(0, rows // step_rows, act_rows, 0)
    h_up.wait_recv()
    h_dn.wait_recv()
    before = act(halo[0].astype(F32))[8:16, :] * jnp.where(s > 0, 1.0, 0.0).astype(F32)
    after = act(halo[1].astype(F32))[0:8, :] * jnp.where(s < S - 1, 1.0, 0.0).astype(F32)
    for j in range(width // 128):
        cols = slice(j * 128, (j + 1) * 128)
        pad[j, 0:8, :] = before[:, cols]
        pad[j, rows + 8:rows + 16, :] = after[:, cols]
        for b in range(taps + 1):
            stack[b * toks:(b + 1) * toks, cols] = pad[
                j, pl.ds(6 + b, toks, stride=2), :
            ].astype(BF16)

    events = {1: (lambda: phase2(0), lambda: phase2(1), lambda: phase1(2)),
              3: (lambda: phase3(0), lambda: phase3(1)),
              4: (lambda: phase4(0), lambda: phase4(1))}
    for n in range(n_tiles):
        cw_copies[n].wait()
        acc[...] = jnp.broadcast_to(vecs[1:2, n * TILE:(n + 1) * TILE], acc.shape)

        def tap(t, carry):
            acc[...] += jnp.dot(
                stack[pl.ds(al(t * toks, 16), 2 * toks), :], cw[n, t], preferred_element_type=F32
            )
            return carry

        lax.fori_loop(0, taps, tap, 0)
        for i in range(TILE // 128):
            j = n * TILE // 128 + i
            part = slice(i * 128, (i + 1) * 128)
            even = resid[j, pl.ds(0, toks, stride=2), :] + acc[0:toks, part]
            odd = resid[j, pl.ds(1, toks, stride=2), :] + acc[toks:2 * toks, part]
            skip[:, j * 128:(j + 1) * 128] = jnp.maximum(even, odd).astype(BF16)
        for e in events.get(n, ()):
            e()


    def norm_rows(i, carry):
        at = pl.ds(al(i * 16, 16), 16)
        v = skip[at, :].astype(F32)
        scale = lax.rsqrt(jnp.mean(v * v, axis=-1, keepdims=True) + 1e-06)
        normed[at, :] = (v * scale * vecs[2:3, :]).astype(BF16)
        return carry

    lax.fori_loop(0, toks // 16, norm_rows, 0)

    cosine = cos_ref[...]
    sine = sin_ref[...]

    def rotate(v):
        return v * cosine + pltpu.roll(v, DK // 2, 1) * sine

    ready(0)
    projected = jnp.dot(normed[...], wkv[...], preferred_element_type=F32)
    own_k[...] = rotate(projected[:, 0:DK]).astype(BF16)
    own_v[0:dv, :] = jnp.transpose(projected[:, DK:]).astype(BF16)
    own_v[dv:, :] = jnp.ones((own_v.shape[0] - dv, toks), BF16)
    mine = (kbuf.at[s], vbuf.at[s])
    own_copies = []
    for i, (a, b) in enumerate(zip((own_k, own_v), mine)):
        cp = pltpu.make_async_copy(a, b, loc_sem.at[3 + i])
        cp.start()
        own_copies.append(cp)
    for cp in own_copies:
        cp.wait()
    kp, kd = {}, {}
    for i, a in enumerate(mine):
        kp[0, i] = start(remote(a, a, kp_s.at[i, 0], kp_r.at[i, 0], (d, partner)))
    for k in range(1, Z):
        for i, a in enumerate(mine):
            kd[k, i] = start(remote(a, a, kd_s.at[i, k - 1], kd_r.at[i, k - 1], (d, fwd(k))))

    ready(1)
    for h in range(HEADS // 2):
        both = jnp.dot(
            normed[...], wq[:, 2 * h * DK:(2 * h + 2) * DK], preferred_element_type=F32
        )
        queries[2 * h] = rotate(both[:, 0:DK]).astype(BF16)
        queries[2 * h + 1] = rotate(both[:, DK:]).astype(BF16)
    phase2(2)

    factor = DK ** (-0.5) * 1.4426950408889634
    for k in range(Z):
        for i, buf in enumerate((kbuf, vbuf)):
            if k > 0:
                kd[k, i].wait_recv()
                at = buf.at[src(k)]
                kp[k, i] = start(remote(at, at, kp_s.at[i, k], kp_r.at[i, k], (d, partner)))
        for i in range(2):
            kp[k, i].wait_recv()
        first = k == 0
        base = ((z + Z - k) % Z) * 2

        def head(h):
            scores = [
                lax.dot_general(
                    kbuf[base + j], queries[h], (((1,), (1,)), ((), ())), preferred_element_type=F32
                )
                for j in range(2)
            ]
            top = jnp.max(jnp.maximum(scores[0], scores[1]), axis=0, keepdims=True)
            if not first:
                old = peak[h][0:1, :]
                top = jnp.maximum(old, top)
            got = None
            for j in range(2):
                weights = jnp.exp2((scores[j] - top) * factor).astype(BF16)
                part = jnp.dot(vbuf[base + j], weights, preferred_element_type=F32)
                got = part if got is None else got + part
            if not first:
                got = got + attn[h] * jnp.exp2((old - top) * factor)
            attn[h] = got
            peak[h] = jnp.broadcast_to(top, (8, toks))

        def heads(i, carry):
            for u in range(UNROLL):
                head(i * UNROLL + u)
            return carry

        lax.fori_loop(0, HEADS // UNROLL, heads, 0)
        if k == 0:
            phase3(2)
        if k == 1:
            phase4(2)

    for h in range(HEADS):
        a = attn[h]
        mixed[:, h * dv:(h + 1) * dv] = jnp.transpose(a[0:dv, :] / a[dv:dv + 1, :]).astype(BF16)

    ready(2)

    outs = []
    for n in range(n_tiles):
        cols = slice(n * TILE, (n + 1) * TILE)
        got = jnp.dot(mixed[...], wo[:, cols], preferred_element_type=F32)
        outv[:, cols] = (skip[:, cols].astype(F32) + got).astype(BF16)
    for cp in sent:
        cp.wait_send()


def body(mesh, section_input, conv_gain, conv_weight, conv_bias, attn_gain, q_weight, kv_weight, o_weight):
    D, S = mesh.shape["dp"], mesh.shape["seq"]
    Z = S // 2
    rows, width = section_input.shape
    toks = rows // 2
    R = q_weight.shape[0]
    G = pieces_of(D, R)
    taps = conv_weight.shape[0]
    nq, nkv, hv = q_weight.shape[1], kv_weight.shape[1], R * S
    dv = nkv - DK
    positions = lax.axis_index("seq") * toks + jnp.arange(toks, dtype=jnp.int32)
    half = DK // 2
    freqs = jnp.power(10000.0, -(jnp.arange(DK, dtype=jnp.int32) % half).astype(F32) / half)
    angle = positions.astype(F32)[:, None] * freqs[None, :]
    cosine = jnp.cos(angle)
    sine = jnp.sin(angle) * jnp.where(jnp.arange(DK) < half, -1.0, 1.0).astype(F32)
    anys = pl.BlockSpec(memory_space=pl.ANY)
    vmem = pl.BlockSpec(memory_space=pltpu.VMEM)
    dma = pltpu.SemaphoreType.DMA
    z1 = max(Z - 1, 1)
    return pl.pallas_call(
        functools.partial(kernel, (D, S, G, R)),
        out_shape=(
            pltpu.VMEM((toks, width), BF16),
            pltpu.VMEM((toks, width), BF16),
        ),
        in_specs=[anys, vmem, anys, vmem, vmem, anys, anys, anys, vmem, vmem],
        out_specs=(vmem, vmem),
        scratch_shapes=[
            pltpu.VMEM((rows, width), BF16),
            pltpu.VMEM((2, 16, width), BF16),
            pltpu.VMEM((width // 128, rows, 128), F32),
            pltpu.VMEM((width // 128, rows + 16, 128), F32),
            pltpu.VMEM(((taps + 1) * toks, width), BF16),
            pltpu.VMEM((width // TILE, taps, width, TILE), BF16),
            pltpu.VMEM((rows, TILE), F32),
            pltpu.VMEM((toks, width), BF16),
            pltpu.VMEM((R * S, nq), BF16),
            pltpu.VMEM((R * S, nkv), BF16),
            pltpu.VMEM((R * S, width), BF16),
            pltpu.VMEM((toks, DK), BF16),
            pltpu.VMEM((dv + 16, toks), BF16),
            pltpu.VMEM((S, toks, DK), BF16),
            pltpu.VMEM((S, dv + 16, toks), BF16),
            pltpu.VMEM((HEADS, toks, DK), BF16),
            pltpu.VMEM((HEADS, 8, toks), F32),
            pltpu.VMEM((HEADS, dv + 16, toks), F32),
            pltpu.VMEM((toks, hv), BF16),
            pltpu.VMEM((8, width), F32),
            dma, dma((width // TILE,)), dma((5,)),
            dma((2,)), dma((2,)),
            dma((3, z1)), dma((3, z1)), dma((3, z1)), dma((3, z1)),
            dma((3, z1, 2)), dma((3, z1, 2)), dma((3, Z)), dma((3, Z)),
            dma((2, z1)), dma((2, z1)), dma((2, Z)), dma((2, Z)),
        ],
        compiler_params=pltpu.CompilerParams(
            collective_id=0, vmem_limit_bytes=58 * 1000 * 1000
        ),
        name="block",
    )(
        section_input, conv_gain, conv_weight, conv_bias, attn_gain, q_weight, kv_weight, o_weight,
        cosine, sine,
    )


def solution(mesh):
    row = P(("dp", "seq"), None)
    seq = P("seq", None)
    in_specs = (row, P(), P(), P(), P(), seq, seq, seq)
    return jax.shard_map(
        functools.partial(body, mesh), mesh=mesh, in_specs=in_specs, out_specs=(row, row), check_vma=False
    )
```

```python
import functools

import jax
import jax.numpy as jnp
from jax import lax
from jax.experimental import pallas as pl
from jax.experimental.pallas import tpu as pltpu
from jax.sharding import PartitionSpec as P

HEADS = 8
DK = 128
TILE = 256
UNROLL = 4
F32 = jnp.float32
BF16 = jnp.bfloat16
MESH = pl.DeviceIdType.MESH


def pieces_of(dp, rows):
    for g in (4, 2):
        if dp % g == 0 and rows % (16 * g) == 0:
            return g
    return 1


def kernel(
    cfg, x_hbm, cgain, cw_hbm, cbias, again, q_hbm, kv_hbm, o_hbm, cos_ref, sin_ref,
    skip, outv,
    xin, halo, resid, pad, stack, cw, acc, normed, wq, wkv, wo, own_k, own_v, kbuf, vbuf, queries,
    peak, attn, mixed, vecs,
    in_sem, cw_sem, loc_sem, halo_s, halo_r, p1_s, p1_r, p2_s, p2_r, p3_s, p3_r, p4_s, p4_r,
    kd_s, kd_r, kp_s, kp_r,
):
    D, S, G, R = cfg
    Z = S // 2
    rows, width = xin.shape
    toks = rows // 2
    n_tiles = width // TILE
    taps = cw.shape[1]
    dv = kv_hbm.shape[1] - DK
    d = lax.axis_index("dp")
    s = lax.axis_index("seq")
    c = lax.rem(s, 2)
    z = s // 2
    partner = s + 1 - 2 * c
    rp = R // G
    me = d % G
    if G == 4:
        f1 = d + 1 - 2 * (d % 2)
        f2 = d + 2 - 4 * ((d // 2) % 2)
        ax1 = f1 + c * (f2 - f1)
        ax2 = f2 + c * (f1 - f2)
    elif G == 2:
        ax1 = d + 1 - 2 * (d % 2)
        ax2 = None
    else:
        ax1 = ax2 = None

    up = (s + 1) % S
    down = (s + S - 1) % S

    def fwd(k):
        return ((z + k) % Z) * 2 + c

    def src(k):
        return ((z + Z - k) % Z) * 2 + c

    in_copy = pltpu.make_async_copy(x_hbm, xin, in_sem)
    in_copy.start()
    cw_copies = []
    for n in range(n_tiles):
        cp = pltpu.make_async_copy(
            cw_hbm.at[:, :, pl.ds(n * TILE, TILE)], cw.at[n], cw_sem.at[n]
        )
        if n < 2:
            cp.start()
        cw_copies.append(cp)

    greet = [(d, up), (d, down), (d, partner)] + [(d, fwd(k)) for k in range(1, Z)]
    if ax1 is not None:
        greet.append((ax1, s))
    if ax2 is not None:
        greet.append((ax2, s))
    bar = pltpu.get_barrier_semaphore()
    for g in greet:
        pl.semaphore_signal(bar, inc=1, device_id=g, device_id_type=MESH)
    pl.semaphore_wait(bar, len(greet))

    def remote(a, b, ss, rs, dev):
        return pltpu.make_async_remote_copy(
            src_ref=a, dst_ref=b, send_sem=ss, recv_sem=rs, device_id=dev, device_id_type=MESH
        )

    sent = []

    def start(cp):
        cp.start()
        sent.append(cp)
        return cp

    h_up = start(remote(x_hbm.at[pl.ds(rows - 16, 16)], halo.at[0], halo_s.at[0], halo_r.at[0], (d, up)))
    h_dn = start(remote(x_hbm.at[pl.ds(0, 16)], halo.at[1], halo_s.at[1], halo_r.at[1], (d, down)))

    hbms = (kv_hbm, q_hbm, o_hbm)
    bufs = (wkv, wq, wo)

    def al(v, m):
        return pl.multiple_of(v, m)

    ph1, ph2, ph3, ph4, locs = {}, {}, {}, {}, {}

    def phase1(a):
        for k in range(1, Z):
            at = pl.ds(al(me * rp, 16), rp)
            to = pl.ds(al(s * R + me * rp, 16), rp)
            ph1[a, k] = start(remote(
                hbms[a].at[at], bufs[a].at[to], p1_s.at[a, k - 1], p1_r.at[a, k - 1], (d, fwd(k))
            ))
        whole = pl.ds(al(s * R, 16), R)
        ph4[a, 0] = start(remote(
            hbms[a], bufs[a].at[whole], p4_s.at[a, 0], p4_r.at[a, 0], (d, partner)
        ))
        locs[a] = pltpu.make_async_copy(hbms[a], bufs[a].at[whole], loc_sem.at[a])
        locs[a].start()

    def phase2(a):
        for k in range(1, Z):
            ph1[a, k].wait_recv()
            if ax1 is not None:
                at = bufs[a].at[pl.ds(al(src(k) * R + me * rp, 16), rp)]
                ph2[a, k] = start(remote(at, at, p2_s.at[a, k - 1], p2_r.at[a, k - 1], (ax1, s)))

    def phase3(a):
        for k in range(1, Z):
            if ax1 is not None:
                ph2[a, k].wait_recv()
            if ax2 is not None:
                for i, piece in enumerate((me, ax1 % G)):
                    at = bufs[a].at[pl.ds(al(src(k) * R + piece * rp, 16), rp)]
                    ph3[a, k, i] = start(remote(
                        at, at, p3_s.at[a, k - 1, i], p3_r.at[a, k - 1, i], (ax2, s)
                    ))

    def phase4(a):
        for k in range(1, Z):
            if ax2 is not None:
                ph3[a, k, 0].wait_recv()
                ph3[a, k, 1].wait_recv()
            at = bufs[a].at[pl.ds(al(src(k) * R, 16), R)]
            ph4[a, k] = start(remote(at, at, p4_s.at[a, k], p4_r.at[a, k], (d, partner)))

    def ready(a):
        locs[a].wait()
        for k in range(Z):
            ph4[a, k].wait_recv()

    phase1(0)
    phase1(1)

    for i, vec in enumerate((cgain, cbias, again)):
        vecs[i:i + 1, :] = vec[...].reshape(1, width)

    def act(v):
        scale = lax.rsqrt(jnp.mean(v * v, axis=-1, keepdims=True) + 1e-06)
        return jax.nn.gelu(v * scale * vecs[0:1, :], approximate=True)

    in_copy.wait()
    step_rows = 16

    def act_rows(i, carry):
        at = al(i * step_rows, step_rows)
        v = xin[pl.ds(at, step_rows), :].astype(F32)
        a = act(v)
        for j in range(width // 128):
            resid[j, pl.ds(at, step_rows), :] = v[:, j * 128:(j + 1) * 128]
            pad[j, pl.ds(al(8 + i * step_rows, 8), step_rows), :] = a[:, j * 128:(j + 1) * 128]
        return carry

    lax.fori_loop(0, rows // step_rows, act_rows, 0)
    h_up.wait_recv()
    h_dn.wait_recv()
    before = act(halo[0].astype(F32))[8:16, :] * jnp.where(s > 0, 1.0, 0.0).astype(F32)
    after = act(halo[1].astype(F32))[0:8, :] * jnp.where(s < S - 1, 1.0, 0.0).astype(F32)
    for j in range(width // 128):
        cols = slice(j * 128, (j + 1) * 128)
        pad[j, 0:8, :] = before[:, cols]
        pad[j, rows + 8:rows + 16, :] = after[:, cols]
        for b in range(taps + 1):
            stack[b * toks:(b + 1) * toks, cols] = pad[
                j, pl.ds(6 + b, toks, stride=2), :
            ].astype(BF16)

    events = {0: (lambda: phase2(0), lambda: phase2(1)),
              2: (lambda: phase3(0), lambda: phase3(1), lambda: phase1(2)),
              4: (lambda: phase4(0), lambda: phase4(1), lambda: phase2(2))}
    for n in range(n_tiles):
        cw_copies[n].wait()
        if n + 2 < n_tiles:
            cw_copies[n + 2].start()
        acc[...] = jnp.broadcast_to(vecs[1:2, n * TILE:(n + 1) * TILE], acc.shape)

        def tap(t, carry):
            acc[...] += jnp.dot(
                stack[pl.ds(al(t * toks, 16), 2 * toks), :], cw[n, t], preferred_element_type=F32
            )
            return carry

        lax.fori_loop(0, taps, tap, 0)
        for i in range(TILE // 128):
            j = n * TILE // 128 + i
            part = slice(i * 128, (i + 1) * 128)
            even = resid[j, pl.ds(0, toks, stride=2), :] + acc[0:toks, part]
            odd = resid[j, pl.ds(1, toks, stride=2), :] + acc[toks:2 * toks, part]
            skip[:, j * 128:(j + 1) * 128] = jnp.maximum(even, odd).astype(BF16)
        for e in events.get(n, ()):
            e()


    def norm_rows(i, carry):
        at = pl.ds(al(i * 16, 16), 16)
        v = skip[at, :].astype(F32)
        scale = lax.rsqrt(jnp.mean(v * v, axis=-1, keepdims=True) + 1e-06)
        normed[at, :] = (v * scale * vecs[2:3, :]).astype(BF16)
        return carry

    lax.fori_loop(0, toks // 16, norm_rows, 0)

    cosine = cos_ref[...]
    sine = sin_ref[...]

    def rotate(v):
        return v * cosine + pltpu.roll(v, DK // 2, 1) * sine

    ready(0)
    projected = jnp.dot(normed[...], wkv[...], preferred_element_type=F32)
    own_k[...] = rotate(projected[:, 0:DK]).astype(BF16)
    own_v[0:dv, :] = jnp.transpose(projected[:, DK:]).astype(BF16)
    own_v[dv:, :] = jnp.ones((own_v.shape[0] - dv, toks), BF16)
    mine = (kbuf.at[s], vbuf.at[s])
    own_copies = []
    for i, (a, b) in enumerate(zip((own_k, own_v), mine)):
        cp = pltpu.make_async_copy(a, b, loc_sem.at[3 + i])
        cp.start()
        own_copies.append(cp)
    for cp in own_copies:
        cp.wait()
    kp, kd = {}, {}
    for i, a in enumerate(mine):
        kp[0, i] = start(remote(a, a, kp_s.at[i, 0], kp_r.at[i, 0], (d, partner)))
    for k in range(1, Z):
        for i, a in enumerate(mine):
            kd[k, i] = start(remote(a, a, kd_s.at[i, k - 1], kd_r.at[i, k - 1], (d, fwd(k))))

    ready(1)
    for h in range(HEADS // 2):
        both = jnp.dot(
            normed[...], wq[:, 2 * h * DK:(2 * h + 2) * DK], preferred_element_type=F32
        )
        queries[2 * h] = rotate(both[:, 0:DK]).astype(BF16)
        queries[2 * h + 1] = rotate(both[:, DK:]).astype(BF16)

    factor = DK ** (-0.5) * 1.4426950408889634
    for k in range(Z):
        for i, buf in enumerate((kbuf, vbuf)):
            if k > 0:
                kd[k, i].wait_recv()
                at = buf.at[src(k)]
                kp[k, i] = start(remote(at, at, kp_s.at[i, k], kp_r.at[i, k], (d, partner)))
        for i in range(2):
            kp[k, i].wait_recv()
        first = k == 0
        base = ((z + Z - k) % Z) * 2

        def head(h):
            scores = [
                lax.dot_general(
                    kbuf[base + j], queries[h], (((1,), (1,)), ((), ())), preferred_element_type=F32
                )
                for j in range(2)
            ]
            top = jnp.max(jnp.maximum(scores[0], scores[1]), axis=0, keepdims=True)
            if not first:
                old = peak[h][0:1, :]
                top = jnp.maximum(old, top)
            got = None
            for j in range(2):
                weights = jnp.exp2((scores[j] - top) * factor).astype(BF16)
                part = jnp.dot(vbuf[base + j], weights, preferred_element_type=F32)
                got = part if got is None else got + part
            if not first:
                got = got + attn[h] * jnp.exp2((old - top) * factor)
            attn[h] = got
            peak[h] = jnp.broadcast_to(top, (8, toks))

        def heads(i, carry):
            for u in range(UNROLL):
                head(i * UNROLL + u)
            return carry

        lax.fori_loop(0, HEADS // UNROLL, heads, 0)
        if k == 0:
            phase3(2)
        if k == 1:
            phase4(2)

    for h in range(HEADS):
        a = attn[h]
        mixed[:, h * dv:(h + 1) * dv] = jnp.transpose(a[0:dv, :] / a[dv:dv + 1, :]).astype(BF16)

    ready(2)

    outs = []
    for n in range(n_tiles):
        cols = slice(n * TILE, (n + 1) * TILE)
        got = jnp.dot(mixed[...], wo[:, cols], preferred_element_type=F32)
        outv[:, cols] = (skip[:, cols].astype(F32) + got).astype(BF16)
    for cp in sent:
        cp.wait_send()


def body(mesh, section_input, conv_gain, conv_weight, conv_bias, attn_gain, q_weight, kv_weight, o_weight):
    D, S = mesh.shape["dp"], mesh.shape["seq"]
    Z = S // 2
    rows, width = section_input.shape
    toks = rows // 2
    R = q_weight.shape[0]
    G = pieces_of(D, R)
    taps = conv_weight.shape[0]
    nq, nkv, hv = q_weight.shape[1], kv_weight.shape[1], R * S
    dv = nkv - DK
    positions = lax.axis_index("seq") * toks + jnp.arange(toks, dtype=jnp.int32)
    half = DK // 2
    freqs = jnp.power(10000.0, -(jnp.arange(DK, dtype=jnp.int32) % half).astype(F32) / half)
    angle = positions.astype(F32)[:, None] * freqs[None, :]
    cosine = jnp.cos(angle)
    sine = jnp.sin(angle) * jnp.where(jnp.arange(DK) < half, -1.0, 1.0).astype(F32)
    anys = pl.BlockSpec(memory_space=pl.ANY)
    vmem = pl.BlockSpec(memory_space=pltpu.VMEM)
    dma = pltpu.SemaphoreType.DMA
    z1 = max(Z - 1, 1)
    return pl.pallas_call(
        functools.partial(kernel, (D, S, G, R)),
        out_shape=(
            pltpu.VMEM((toks, width), BF16),
            pltpu.VMEM((toks, width), BF16),
        ),
        in_specs=[anys, vmem, anys, vmem, vmem, anys, anys, anys, vmem, vmem],
        out_specs=(vmem, vmem),
        scratch_shapes=[
            pltpu.VMEM((rows, width), BF16),
            pltpu.VMEM((2, 16, width), BF16),
            pltpu.VMEM((width // 128, rows, 128), F32),
            pltpu.VMEM((width // 128, rows + 16, 128), F32),
            pltpu.VMEM(((taps + 1) * toks, width), BF16),
            pltpu.VMEM((width // TILE, taps, width, TILE), BF16),
            pltpu.VMEM((rows, TILE), F32),
            pltpu.VMEM((toks, width), BF16),
            pltpu.VMEM((R * S, nq), BF16),
            pltpu.VMEM((R * S, nkv), BF16),
            pltpu.VMEM((R * S, width), BF16),
            pltpu.VMEM((toks, DK), BF16),
            pltpu.VMEM((dv + 16, toks), BF16),
            pltpu.VMEM((S, toks, DK), BF16),
            pltpu.VMEM((S, dv + 16, toks), BF16),
            pltpu.VMEM((HEADS, toks, DK), BF16),
            pltpu.VMEM((HEADS, 8, toks), F32),
            pltpu.VMEM((HEADS, dv + 16, toks), F32),
            pltpu.VMEM((toks, hv), BF16),
            pltpu.VMEM((8, width), F32),
            dma, dma((width // TILE,)), dma((5,)),
            dma((2,)), dma((2,)),
            dma((3, z1)), dma((3, z1)), dma((3, z1)), dma((3, z1)),
            dma((3, z1, 2)), dma((3, z1, 2)), dma((3, Z)), dma((3, Z)),
            dma((2, z1)), dma((2, z1)), dma((2, Z)), dma((2, Z)),
        ],
        compiler_params=pltpu.CompilerParams(
            collective_id=0, vmem_limit_bytes=58 * 1000 * 1000
        ),
        name="block",
    )(
        section_input, conv_gain, conv_weight, conv_bias, attn_gain, q_weight, kv_weight, o_weight,
        cosine, sine,
    )


def solution(mesh):
    row = P(("dp", "seq"), None)
    seq = P("seq", None)
    in_specs = (row, P(), P(), P(), P(), seq, seq, seq)
    return jax.shard_map(
        functools.partial(body, mesh), mesh=mesh, in_specs=in_specs, out_specs=(row, row), check_vma=False
    )
```
